32 devices in a mesh: section: 2 (over core), shard: 4 (over y, x), replica: 4 (over z).
Axes of the slice: x: 2, y: 2, z: 4, core: 2. Of those that a mesh axis runs over, the one named last changes fastest.
Arguments:
- inputs: bfloat16 [8, 256, 960], P('replica', 'shard'), may hold values from -6 to 6
- cotangent: bfloat16 [8, 256, 960], P('replica', 'shard'), may hold values from -6 to 6
- segments: int32 [8, 256], P('replica'), may hold values from 0 to 3, never falling along the last dimension, each value on 1 to 128 neighbouring positions
- attn_q: bfloat16 [2, 960, 960], P('section', None, 'shard'), may hold values from -0.1875 to 0.1875
- attn_k: bfloat16 [2, 960, 320], P('section', None, 'shard'), may hold values from -0.1875 to 0.1875
- attn_v: bfloat16 [2, 960, 320], P('section', None, 'shard'), may hold values from -0.1875 to 0.1875
- attn_out: bfloat16 [2, 960, 960], P('section', None, 'shard'), may hold values from -0.75 to 0.75
- ffn_gate: bfloat16 [2, 960, 2560], P('section', None, 'shard'), may hold values from -0.1875 to 0.1875
- ffn_up: bfloat16 [2, 960, 2560], P('section', None, 'shard'), may hold values from -0.1875 to 0.1875
- ffn_down: bfloat16 [2, 2560, 960], P('section', 'shard'), may hold values from -0.125 to 0.125
- norm_gains: float32 [2, 2, 960], P('section'), may hold values from 0.1 to 1.9
Outputs:
- activations: bfloat16 [2, 8, 256, 960], P('section', 'replica', 'shard')
- input_grads: bfloat16 [2, 8, 256, 960], P('section', 'replica', 'shard')
- grad_q: float32 [2, 960, 960], P('section', 'replica', 'shard')
- grad_k: float32 [2, 960, 320], P('section', 'replica', 'shard')
- grad_v: float32 [2, 960, 320], P('section', 'replica', 'shard')
- grad_out: float32 [2, 960, 960], P('section', 'replica', 'shard')
- grad_gate: float32 [2, 960, 2560], P('section', 'replica', 'shard')
- grad_up: float32 [2, 960, 2560], P('section', 'replica', 'shard')
- grad_down: float32 [2, 2560, 960], P('section', 'shard', 'replica')
- grad_gains: float32 [2, 2, 960], P('section')
The draws below stay inside these ranges and needn't reach their ends.
Inputs may be any that keep to these rules, and one draw needn't show every extreme that they name: `segments`: segment numbers never fall along a row, and every one of the 4 numbers occurs in every row.
All inputs are finite; a program needn't handle non-finite values.
Results may differ from the reference program's by a relative error of at most 0.024.
Values may be sent and summed in bfloat16 or wider, within the bound.
No kernel may reach another device: no remote copies, remote signals or barrier semaphores. Data moves between devices by JAX's collectives and lax.ppermute only.
A program may use at most 128 MiB of HBM per device.

```python
import math
import jax
import jax.numpy as jnp
import numpy as np
from jax import lax

D = 960
HQ = 15
KV = 5
HD = 64
FF = 2560
SEQ = 256
MICRO = 2
DOCS = 4
ROWS = 8


def block_levels(key, shape, cuts, smallest, high):
    gain, own = 1.0, jax.random.fold_in(key, 6)
    for dim, shards_of in cuts:
        steps = jnp.exp(jax.random.uniform(jax.random.fold_in(own, dim), (shards_of,), jnp.float32, smallest / len(cuts), high / len(cuts)))
        gain = gain * jnp.repeat(steps, shape[dim] // shards_of).reshape([-1 if axis == dim else 1 for axis in range(len(shape))])
    return gain


def length_profile(count, total, bound, slope):
    weights = [(1 << 20) // math.isqrt(standing ** slope) + 1 for standing in range(2, count + 1)]
    surplus, given = total - bound - (count - 1), [1] * (count - 1)
    while surplus > 0:
        movable = [i for i in range(count - 1) if given[i] < bound]
        pool, budget = sum([weights[i] for i in movable]), surplus
        for i in movable:
            more = min(bound - given[i], max(1, budget * weights[i] // pool), surplus)
            given[i] = given[i] + more
            surplus = surplus - more
    return np.array([bound] + given)


def ragged_sizes(key, number_of, total, most, skew):
    if number_of == 2:
        one = jax.random.randint(key, (), max(1, total - most), min(most, total - 1) + 1)
        return jnp.stack([one, total - one])
    lengths = jnp.asarray(length_profile(number_of, total, most, skew), jnp.int32)
    twos = (number_of - 1) // 2
    giver, sink = lengths[1:1 + 2 * twos:2], lengths[2:2 + 2 * twos:2]
    room = jnp.minimum(giver - 1, most - sink)
    passed = jax.random.randint(jax.random.fold_in(key, 1), (twos,), 0, 1 << 20) % (room + 1)
    lengths = lengths.at[1:1 + 2 * twos:2].set(giver - passed).at[2:2 + 2 * twos:2].set(sink + passed)
    return lengths[jax.random.permutation(jax.random.fold_in(key, 2), number_of)]


def scatter_about(own_key, extent, scale, reach, split=(), kind=jnp.bfloat16):
    array = scale * jax.random.normal(own_key, extent, jnp.float32)
    if split:
        array = array * block_levels(own_key, extent, split, -0.22, 0.18)
    return jnp.clip(array, -reach, reach).astype(kind)


def setup_inputs(seed: int = 0) -> dict:
    key_list = jax.random.split(jax.random.key(seed), 12)
    return {
        "inputs": scatter_about(key_list[0], (ROWS, SEQ, D), 1.0, 6.0, ((0, 4), (1, 4))),
        "cotangent": scatter_about(key_list[1], (ROWS, SEQ, D), 1.0, 6.0, ((0, 4), (1, 4))),
        "segments": jax.vmap(lambda own: jnp.searchsorted(jnp.cumsum(ragged_sizes(own, DOCS, SEQ, SEQ // 2, 1)), jnp.arange(SEQ), side="right"))(jax.random.split(key_list[2], ROWS)).reshape((ROWS, SEQ)).astype(jnp.int32),
        "attn_q": scatter_about(key_list[3], (2, D, HQ * HD), D ** -0.5, 0.1875, ((0, 2), (2, 4))),
        "attn_k": scatter_about(key_list[4], (2, D, KV * HD), D ** -0.5, 0.1875, ((0, 2), (2, 4))),
        "attn_v": scatter_about(key_list[5], (2, D, KV * HD), D ** -0.5, 0.1875, ((0, 2), (2, 4))),
        "attn_out": scatter_about(key_list[6], (2, HQ * HD, D), (HQ * HD // 16) ** -0.5, 0.75, ((0, 2), (2, 4))),
        "ffn_gate": scatter_about(key_list[7], (2, D, FF), D ** -0.5, 0.1875, ((0, 2), (2, 4))),
        "ffn_up": scatter_about(key_list[8], (2, D, FF), D ** -0.5, 0.1875, ((0, 2), (2, 4))),
        "ffn_down": scatter_about(key_list[9], (2, FF, D), FF ** -0.5, 0.125, ((0, 2), (1, 4))),
        "norm_gains": jnp.clip(1.0 + 0.18 * jax.random.normal(key_list[10], (2, 2, D), jnp.float32), 0.1, 1.9),
    }


epsilon = 1e-05
rope_base = 10000.0
masked_score = -1e+30

def matmul(left, right):
    return jnp.dot(left, right, preferred_element_type=jnp.float32)

def rope_tables(segments):
    length = segments.shape[-1]
    position = jnp.arange(length, dtype=jnp.int32)
    before = jnp.concatenate([segments[:, :1] - 1, segments[:, :-1]], axis=1)
    starts = jnp.where(segments != before, position, 0).astype(jnp.int32)
    starts = lax.cummax(starts, axis=1)
    places = (position - starts).astype(jnp.float32)
    frequency = rope_base ** (jnp.arange(HD // 2, dtype=jnp.float32) * (-2.0 / HD))
    angles = places[..., None] * frequency
    return (jnp.cos(angles), jnp.sin(angles))

def allowed_mask(segments):
    length = segments.shape[-1]
    position = jnp.arange(length, dtype=jnp.int32)
    same_doc = segments[:, :, None] == segments[:, None, :]
    return same_doc & (position[:, None] >= position[None, :])[None]

def rotate(values, cosine, sine_table):
    half_dim = values.shape[-1] // 2
    first_half = values[..., :half_dim]
    second_half = values[..., half_dim:]
    return jnp.concatenate([first_half * cosine - second_half * sine_table, second_half * cosine + first_half * sine_table], axis=-1)

def rotate_back(cotang, cosine, sine_table):
    half_dim = cotang.shape[-1] // 2
    first_half = cotang[..., :half_dim]
    second_half = cotang[..., half_dim:]
    return jnp.concatenate([first_half * cosine + second_half * sine_table, second_half * cosine - first_half * sine_table], axis=-1)

def score_block(queries, key_rows, allowed):
    scores = jnp.einsum('gqkrd,gpkd->gkrqp', queries.astype(jnp.float32), key_rows.astype(jnp.float32)) * HD ** (-0.5)
    return jnp.where(allowed[:, None, None], scores, masked_score)

def attend_forward(queries, key_rows, value_rows, allowed):
    scores = score_block(queries, key_rows, allowed)
    row_max = lax.optimization_barrier(jnp.max(scores, axis=-1, keepdims=True))
    log_total = row_max + jnp.log(lax.optimization_barrier(jnp.sum(jnp.exp(scores - row_max), axis=-1, keepdims=True)))
    prob_rows = jnp.exp(scores - log_total).astype(jnp.bfloat16)
    attended = jnp.einsum('gkrqp,gpkd->gqkrd', prob_rows.astype(jnp.float32), value_rows.astype(jnp.float32))
    return (log_total, attended.astype(jnp.bfloat16))

def attend_backward(queries, key_rows, value_rows, allowed, log_total, attended, d_attended):
    scores = score_block(queries, key_rows, allowed)
    prob_full = jnp.exp(scores - log_total)
    prob_rows = prob_full.astype(jnp.bfloat16)
    d_probs = jnp.einsum('gqkrd,gpkd->gkrqp', d_attended.astype(jnp.float32), value_rows.astype(jnp.float32))
    delta = jnp.einsum('gqkrd,gqkrd->gkrq', d_attended.astype(jnp.float32), attended.astype(jnp.float32))
    d_scores = (prob_full * (d_probs - delta[..., None]) * HD ** (-0.5)).astype(jnp.bfloat16)
    d_queries = jnp.einsum('gkrqp,gpkd->gqkrd', d_scores.astype(jnp.float32), key_rows.astype(jnp.float32))
    d_keys = jnp.einsum('gkrqp,gqkrd->gpkd', d_scores.astype(jnp.float32), queries.astype(jnp.float32))
    d_values = jnp.einsum('gkrqp,gqkrd->gpkd', prob_rows.astype(jnp.float32), d_attended.astype(jnp.float32))
    return (d_queries, d_keys, d_values)

def layer_forward(layer_in, segments, weights):
    weight_q, weight_k, weight_v, weight_out, weight_gate, weight_up, weight_down, gain_attn, gain_ffn = weights
    groups, length = segments.shape
    tokens_all = groups * length
    group_size = HQ // KV
    cosine, sine_table = rope_tables(segments)
    cosine = cosine[:, :, None, :]
    sine_table = sine_table[:, :, None, :]
    allowed = allowed_mask(segments)
    inputs_f = layer_in.reshape(tokens_all, D).astype(jnp.float32)
    inv_attn = lax.rsqrt(lax.optimization_barrier(jnp.mean(inputs_f * inputs_f, axis=-1, keepdims=True)) + epsilon)
    normed = (inputs_f * inv_attn * gain_attn).astype(jnp.bfloat16)
    queries = rotate(matmul(normed, weight_q).reshape(groups, length, HQ, HD), cosine, sine_table).astype(jnp.bfloat16)
    queries = queries.reshape(groups, length, KV, group_size, HD)
    key_rows = rotate(matmul(normed, weight_k).reshape(groups, length, KV, HD), cosine, sine_table).astype(jnp.bfloat16)
    value_rows = matmul(normed, weight_v).astype(jnp.bfloat16).reshape(groups, length, KV, HD)
    log_total, attended = attend_forward(queries, key_rows, value_rows, allowed)
    attended_flat = attended.reshape(tokens_all, HQ * HD)
    middle = inputs_f + matmul(attended_flat, weight_out)
    inv_ffn = lax.rsqrt(lax.optimization_barrier(jnp.mean(middle * middle, axis=-1, keepdims=True)) + epsilon)
    normed_ffn = (middle * inv_ffn * gain_ffn).astype(jnp.bfloat16)
    gate_pre = matmul(normed_ffn, weight_gate)
    up_pre = matmul(normed_ffn, weight_up)
    hidden = (jax.nn.silu(gate_pre) * up_pre).astype(jnp.bfloat16)
    layer_out = (middle + matmul(hidden, weight_down)).astype(jnp.bfloat16)
    saved = (inputs_f, inv_attn, normed, queries, key_rows, value_rows, log_total, attended, middle, inv_ffn, normed_ffn, gate_pre, up_pre, hidden)
    return (layer_out.reshape(groups, length, D), saved)

def layer_backward(upstream_in, segments, weights, saved):
    weight_q, weight_k, weight_v, weight_out, weight_gate, weight_up, weight_down, gain_attn, gain_ffn = weights
    inputs_f, inv_attn, normed, queries, key_rows, value_rows, log_total, attended, middle, inv_ffn, normed_ffn, gate_pre, up_pre, hidden = saved
    groups, length = segments.shape
    tokens_all = groups * length
    group_size = HQ // KV
    cosine, sine_table = rope_tables(segments)
    cosine = cosine[:, :, None, :]
    sine_table = sine_table[:, :, None, :]
    allowed = allowed_mask(segments)
    upstream = upstream_in.reshape(tokens_all, D)
    d_hidden = matmul(upstream, weight_down.T)
    sigma = jax.nn.sigmoid(gate_pre)
    d_gate = (d_hidden * up_pre * sigma * (1.0 + gate_pre * (1.0 - sigma))).astype(jnp.bfloat16)
    d_up = (d_hidden * gate_pre * sigma).astype(jnp.bfloat16)
    d_normed_ffn = matmul(d_gate, weight_gate.T) + matmul(d_up, weight_up.T)
    scaled_ffn = d_normed_ffn * gain_ffn
    d_middle = upstream.astype(jnp.float32) + inv_ffn * scaled_ffn - middle * (inv_ffn * inv_ffn * inv_ffn) * lax.optimization_barrier(jnp.mean(scaled_ffn * middle, axis=-1, keepdims=True))
    d_middle_b = d_middle.astype(jnp.bfloat16)
    d_attended = matmul(d_middle_b, weight_out.T).astype(jnp.bfloat16).reshape(groups, length, KV, group_size, HD)
    d_queries, d_keys, d_values = attend_backward(queries, key_rows, value_rows, allowed, log_total, attended, d_attended)
    d_q_rot = rotate_back(d_queries.reshape(groups, length, HQ, HD), cosine, sine_table).reshape(tokens_all, HQ * HD).astype(jnp.bfloat16)
    d_k_rot = rotate_back(d_keys, cosine, sine_table).reshape(tokens_all, KV * HD).astype(jnp.bfloat16)
    d_v_rows = d_values.reshape(tokens_all, KV * HD).astype(jnp.bfloat16)
    d_normed = matmul(d_q_rot, weight_q.T) + matmul(d_k_rot, weight_k.T) + matmul(d_v_rows, weight_v.T)
    scaled_attn = d_normed * gain_attn
    d_inputs = d_middle + inv_attn * scaled_attn - inputs_f * (inv_attn * inv_attn * inv_attn) * lax.optimization_barrier(jnp.mean(scaled_attn * inputs_f, axis=-1, keepdims=True))
    d_inputs = d_inputs.astype(jnp.bfloat16).reshape(groups, length, D)
    attended_flat = attended.reshape(tokens_all, HQ * HD)
    gain_terms = jnp.stack([lax.optimization_barrier(jnp.sum(d_normed * inputs_f * inv_attn, axis=0)), lax.optimization_barrier(jnp.sum(d_normed_ffn * middle * inv_ffn, axis=0))])
    grads = (matmul(normed.T, d_q_rot), matmul(normed.T, d_k_rot), matmul(normed.T, d_v_rows), matmul(attended_flat.T, d_middle_b), matmul(normed_ffn.T, d_gate), matmul(normed_ffn.T, d_up), matmul(hidden.T, upstream), gain_terms)
    return (d_inputs, grads)

def rounded_group(grads):
    return tuple(grads)

def zero_grads():
    return (jnp.zeros((D, HQ * HD), jnp.float32), jnp.zeros((D, KV * HD), jnp.float32), jnp.zeros((D, KV * HD), jnp.float32), jnp.zeros((HQ * HD, D), jnp.float32), jnp.zeros((D, FF), jnp.float32), jnp.zeros((D, FF), jnp.float32), jnp.zeros((FF, D), jnp.float32), jnp.zeros((2, D), jnp.float32))

def reference(inputs, cotangent, segments, attn_q, attn_k, attn_v, attn_out, ffn_gate, ffn_up, ffn_down, norm_gains):
    block_count = ROWS // MICRO
    layer_one = (attn_q[0], attn_k[0], attn_v[0], attn_out[0], ffn_gate[0], ffn_up[0], ffn_down[0], norm_gains[0, 0], norm_gains[0, 1])
    layer_two = (attn_q[1], attn_k[1], attn_v[1], attn_out[1], ffn_gate[1], ffn_up[1], ffn_down[1], norm_gains[1, 0], norm_gains[1, 1])

    def one_block(running, block_in):
        x_block, cot_block, seg_block = block_in
        middle_acts, saved_one = layer_forward(x_block, seg_block, layer_one)
        final_acts, saved_two = layer_forward(middle_acts, seg_block, layer_two)
        d_middle_acts, grads_two = layer_backward(cot_block, seg_block, layer_two, saved_two)
        d_first, grads_one = layer_backward(d_middle_acts, seg_block, layer_one, saved_one)
        addition = (rounded_group(grads_one), rounded_group(grads_two))
        running = jax.tree.map(lambda before_sum, addend: before_sum + addend, running, addition)
        return (running, (middle_acts, final_acts, d_first, d_middle_acts))
    blocks = (inputs.reshape(block_count, MICRO, SEQ, D), cotangent.reshape(block_count, MICRO, SEQ, D), segments.reshape(block_count, MICRO, SEQ))
    totals, stacked = lax.scan(one_block, (zero_grads(), zero_grads()), blocks)
    activations = jnp.stack([stacked[0].reshape(ROWS, SEQ, D), stacked[1].reshape(ROWS, SEQ, D)])
    input_grads = jnp.stack([stacked[2].reshape(ROWS, SEQ, D), stacked[3].reshape(ROWS, SEQ, D)])
    outputs = [jnp.stack([totals[0][slot], totals[1][slot]]) for slot in range(8)]
    return (activations, input_grads, outputs[0], outputs[1], outputs[2], outputs[3], outputs[4], outputs[5], outputs[6], outputs[7])
```

```python
import functools

import jax
import jax.numpy as jnp
from jax import lax
from jax.experimental import pallas as pl
from jax.experimental.pallas import tpu as pltpu
from jax.sharding import PartitionSpec as P

HQ = 15
KV = 5
HD = 64
GROUP = HQ // KV
epsilon = 1e-05
rope_base = 10000.0
masked_score = -1e30
F32 = jnp.float32
BF16 = jnp.bfloat16


def dot(left, right):
    return lax.dot_general(left, right, (((1,), (0,)), ((), ())), preferred_element_type=F32)


def dot_nt(left, right):
    return lax.dot_general(left, right, (((1,), (1,)), ((), ())), preferred_element_type=F32)


def dot_tn(left, right):
    return lax.dot_general(left, right, (((0,), (0,)), ((), ())), preferred_element_type=F32)


def wide(table, width):
    copies = -(-width // table.shape[1])
    return jnp.concatenate([table] * copies, axis=1)[:, :width]


def swap_halves(values):
    half = HD // 2
    up = jnp.concatenate([values[:, half:], values[:, :half]], axis=1)
    down = jnp.concatenate([values[:, -half:], values[:, :-half]], axis=1)
    lane = lax.broadcasted_iota(jnp.int32, values.shape, 1)
    return jnp.where(lane % HD < half, up, down)


def rope(values, cosine, sine, sign):
    width = values.shape[1]
    turned = swap_halves(values) * wide(sine, width)
    straight = values * wide(cosine, width)
    return straight + turned if sign > 0 else straight - turned


def forward_kernel(at_ref, u_ref, w_ref, gate_ref, up_ref, down_ref, gain_ref, cos_ref, sin_ref,
                   seg_c_ref, pos_c_ref, seg_r_ref, pos_r_ref,
                   part_ref, normed_ref, q_ref, k_ref, v_ref, prob_ref, att_ref, mid_ref, nffn_ref,
                   gpre_ref, upre_ref, hid_ref, qf_ref, kf_ref):
    at = at_ref[0]
    count = w_ref.shape[0]
    width = u_ref.shape[1]
    qw = HQ * HD // count
    kw = KV * HD // count
    u = u_ref[...].astype(F32)
    inv_a = lax.rsqrt(jnp.mean(u * u, axis=-1, keepdims=True) + epsilon)
    normed = (u * inv_a * gain_ref[0:1, :]).astype(BF16)
    normed_ref[...] = normed
    for c in range(count):
        rc = lax.rem(at - c + count, count)
        qkv = dot(normed, w_ref[rc, :, : qw + 2 * kw])
        qf_ref[:, c * qw : (c + 1) * qw] = qkv[:, :qw]
        kf_ref[:, c * kw : (c + 1) * kw] = qkv[:, qw : qw + kw]
        v_ref[:, c * kw : (c + 1) * kw] = qkv[:, qw + kw :].astype(BF16)
    cosine = cos_ref[...]
    sine = sin_ref[...]
    q_ref[...] = rope(qf_ref[...], cosine, sine, 1).astype(BF16)
    k_ref[...] = rope(kf_ref[...], cosine, sine, 1).astype(BF16)
    allowed = (seg_c_ref[...] == seg_r_ref[...]) & (pos_c_ref[...] >= pos_r_ref[...])
    for h in range(KV):
        keys = k_ref[:, h * HD : (h + 1) * HD]
        vals = v_ref[:, h * HD : (h + 1) * HD]
        for g in range(GROUP):
            hd = h * GROUP + g
            scores = dot_nt(q_ref[:, hd * HD : (hd + 1) * HD], keys) * HD ** (-0.5)
            scores = jnp.where(allowed, scores, masked_score)
            e = jnp.exp(scores - jnp.max(scores, axis=-1, keepdims=True))
            prob = (e / jnp.sum(e, axis=-1, keepdims=True)).astype(BF16)
            prob_ref[hd] = prob
            att_ref[:, hd * HD : (hd + 1) * HD] = dot(prob, vals).astype(BF16)
    attended = att_ref[...]
    cw = width // count
    for c in range(count):
        rc = lax.rem(at - c + count, count)
        mid_ref[:, c * cw : (c + 1) * cw] = dot(attended, w_ref[rc, :, qw + 2 * kw :])
    middle = u + mid_ref[...]
    mid_ref[...] = middle
    inv_f = lax.rsqrt(jnp.mean(middle * middle, axis=-1, keepdims=True) + epsilon)
    nffn = (middle * inv_f * gain_ref[1:2, :]).astype(BF16)
    nffn_ref[...] = nffn
    gpre = dot(nffn, gate_ref[...])
    upre = dot(nffn, up_ref[...])
    gpre_ref[...] = gpre
    upre_ref[...] = upre
    hidden = (gpre * jax.nn.sigmoid(gpre) * upre).astype(BF16)
    hid_ref[...] = hidden
    part_ref[...] = dot(hidden, down_ref[...]).astype(BF16)


def ffn_back_kernel(g_ref, gpre_ref, upre_ref, gate_ref, up_ref, down_ref, dgu_ref, part_ref):
    d_hidden = dot_nt(g_ref[...], down_ref[...])
    gpre = gpre_ref[...]
    sigma = jax.nn.sigmoid(gpre)
    d_gate = (d_hidden * upre_ref[...] * sigma * (1.0 + gpre * (1.0 - sigma))).astype(BF16)
    d_up = (d_hidden * gpre * sigma).astype(BF16)
    hidden = d_gate.shape[1]
    dgu_ref[:, :hidden] = d_gate
    dgu_ref[:, hidden:] = d_up
    part_ref[...] = (dot_nt(d_gate, gate_ref[...]) + dot_nt(d_up, up_ref[...])).astype(BF16)


def attn_back_kernel(at_ref, dmid_ref, u_ref, w_ref, gain_ref, cos_ref, sin_ref, q_ref, k_ref, v_ref,
                     prob_ref, att_ref,
                     din_ref, dqkv_ref, dmo_ref, gsum_ref, datt_ref, dq_ref, dk_ref, dv_ref, piece_ref, *, own):
    at = at_ref[0]
    count = w_ref.shape[0]
    width = u_ref.shape[1]
    qw = HQ * HD // count
    kw = KV * HD // count
    cw = width // count
    dmid = dmid_ref[...]
    d_att = jnp.zeros((dmid.shape[0], HQ * HD), F32)
    for c in range(count):
        rc = lax.rem(at - c + count, count)
        d_att = d_att + dot_nt(dmid[:, c * cw : (c + 1) * cw], w_ref[rc, :, qw + 2 * kw :])

        @pl.when(at == c)
        def _():
            dmo_ref[...] = dmid[:, c * cw : (c + 1) * cw]

    datt_ref[...] = d_att.astype(BF16)
    for h in range(KV):
        keys = k_ref[:, h * HD : (h + 1) * HD]
        vals = v_ref[:, h * HD : (h + 1) * HD]
        d_k = jnp.zeros((dmid.shape[0], HD), F32)
        d_v = jnp.zeros((dmid.shape[0], HD), F32)
        for g in range(GROUP):
            hd = h * GROUP + g
            span = slice(hd * HD, (hd + 1) * HD)
            da = datt_ref[:, span]
            prob = prob_ref[hd]
            d_prob = dot_nt(da, vals)
            delta = jnp.sum(da.astype(F32) * att_ref[:, span].astype(F32), axis=-1, keepdims=True)
            d_s = (prob.astype(F32) * (d_prob - delta) * HD ** (-0.5)).astype(BF16)
            dq_ref[:, span] = dot(d_s, keys)
            d_k = d_k + dot_tn(d_s, q_ref[:, span])
            d_v = d_v + dot_tn(prob, da)
        dk_ref[:, h * HD : (h + 1) * HD] = d_k
        dv_ref[:, h * HD : (h + 1) * HD] = d_v
    cosine = cos_ref[...]
    sine = sin_ref[...]
    d_q = rope(dq_ref[...], cosine, sine, -1)
    d_k = rope(dk_ref[...], cosine, sine, -1)
    d_v = dv_ref[...]
    d_normed = jnp.zeros(dmid.shape, F32)
    for c in range(count):
        rc = lax.rem(at - c + count, count)
        q_span = slice(c * qw, (c + 1) * qw)
        k_span = slice(c * kw, (c + 1) * kw)
        piece_ref[:, :qw] = d_q[:, q_span]
        piece_ref[:, qw : qw + kw] = d_k[:, k_span]
        piece_ref[:, qw + kw :] = d_v[:, k_span]
        piece = piece_ref[...].astype(BF16)
        d_normed = d_normed + dot_nt(piece, w_ref[rc, :, : qw + 2 * kw])

        @pl.when(at == c)
        def _():
            dqkv_ref[...] = piece

    u = u_ref[...].astype(F32)
    inv_a = lax.rsqrt(jnp.mean(u * u, axis=-1, keepdims=True) + epsilon)
    scaled = d_normed * gain_ref[0:1, :]
    d_in = dmid.astype(F32) + inv_a * scaled - u * (inv_a * inv_a * inv_a) * jnp.mean(
        scaled * u, axis=-1, keepdims=True
    )
    din_ref[...] = d_in.astype(BF16)
    gsum_ref[...] = jnp.sum((d_normed * u * inv_a)[:own], axis=0, keepdims=True)


def sds(shape, kind):
    return jax.ShapeDtypeStruct(shape, kind)


def specs(memory, operands):
    return [pl.BlockSpec(memory_space=memory)] + [pl.BlockSpec(memory_space=pltpu.VMEM)] * operands


LIMIT = pltpu.CompilerParams(vmem_limit_bytes=60 * 1024 * 1024)


def run_forward(at, u, weights, gate, up, down, gains, tables):
    t, width = u.shape
    ff = gate.shape[1]
    outs = (
        sds((t, width), BF16), sds((t, width), BF16), sds((t, HQ * HD), BF16), sds((t, KV * HD), BF16),
        sds((t, KV * HD), BF16), sds((HQ, t, t), BF16), sds((t, HQ * HD), BF16), sds((t, width), F32),
        sds((t, width), BF16), sds((t, ff), F32), sds((t, ff), F32), sds((t, ff), BF16),
    )
    return pl.pallas_call(
        forward_kernel,
        out_shape=outs,
        in_specs=specs(pltpu.SMEM, 12),
        scratch_shapes=[pltpu.VMEM((t, HQ * HD), F32), pltpu.VMEM((t, KV * HD), F32)],
        compiler_params=LIMIT,
        name="layer_forward",
    )(at, u, weights, gate, up, down, gains, *tables)


def run_ffn_back(upstream, gpre, upre, gate, up, down):
    t, width = upstream.shape
    ff = gate.shape[1]
    return pl.pallas_call(
        ffn_back_kernel,
        out_shape=(sds((t, 2 * ff), BF16), sds((t, width), BF16)),
        compiler_params=LIMIT,
        name="ffn_backward",
    )(upstream, gpre, upre, gate, up, down)


def run_attn_back(at, dmid, u, weights, gains, cosine, sine, q, k, v, prob, att, own):
    t, width = u.shape
    count = weights.shape[0]
    return pl.pallas_call(
        functools.partial(attn_back_kernel, own=own),
        out_shape=(
            sds((t, width), BF16), sds((t, (HQ + 2 * KV) * HD // count), BF16),
            sds((t, width // count), BF16), sds((1, width), F32),
        ),
        in_specs=specs(pltpu.SMEM, 11),
        scratch_shapes=[
            pltpu.VMEM((t, HQ * HD), BF16), pltpu.VMEM((t, HQ * HD), F32),
            pltpu.VMEM((t, KV * HD), F32), pltpu.VMEM((t, KV * HD), F32),
            pltpu.VMEM((t, (HQ + 2 * KV) * HD // count), F32),
        ],
        compiler_params=LIMIT,
        name="attention_backward",
    )(at, dmid, u, weights, gains, cosine, sine, q, k, v, prob, att)


def from_ahead(block, step, axis="shard"):
    n = lax.axis_size(axis)
    return lax.ppermute(block, axis, [(i, (i - step) % n) for i in range(n)])


def to_ahead(block, step, axis="shard"):
    n = lax.axis_size(axis)
    return lax.ppermute(block, axis, [(i, (i + step) % n) for i in range(n)])


def swap_section(block):
    return lax.ppermute(block, "section", [(0, 1), (1, 0)])


def gather_blocks(block):
    n = lax.axis_size("shard")
    return [block] + [from_ahead(block, i) for i in range(1, n)]


def gather_rows(block):
    return jnp.concatenate(gather_blocks(block), axis=0)


def scatter_rows(part):
    n = lax.axis_size("shard")
    size = part.shape[0] // n
    got = [to_ahead(part[i * size : (i + 1) * size], i) for i in range(1, n)]
    total = part[:size].astype(F32)
    for piece in got:
        total = total + piece.astype(F32)
    return total


def doubled_sum(block, axis):
    n = lax.axis_size(axis)
    step = 1
    while step < n:
        block = block + lax.ppermute(block, axis, [(i, i ^ step) for i in range(n)])
        step *= 2
    return block


def reduce_grad(partial, layer):
    n = lax.axis_size("replica")
    at = lax.axis_index("replica")
    other = lax.ppermute(partial, "section", [(1 - layer, layer)])
    total = partial.astype(F32) + other.astype(F32)
    rows = total.shape[0] // n
    if n > 4:
        return lax.psum_scatter(total.astype(BF16), "replica", scatter_dimension=0, tiled=True).astype(F32)
    sent = total.astype(BF16)
    result = lax.dynamic_slice_in_dim(sent, at * rows, rows, 0).astype(F32)
    for step in range(1, n):
        chunk = lax.dynamic_slice_in_dim(sent, lax.rem(at + step, n) * rows, rows, 0)
        route = [(layer * n + i, layer * n + (i + step) % n) for i in range(n)]
        result = result + lax.ppermute(chunk, ("section", "replica"), route).astype(F32)
    return result


def local(inputs, cotangent, segments, attn_q, attn_k, attn_v, attn_out, ffn_gate, ffn_up, ffn_down, norm_gains):
    section = lax.axis_index("section")
    shard = lax.axis_index("shard")
    n = lax.axis_size("shard")
    block = inputs.shape[1]
    width = inputs.shape[2]
    row_len = segments.shape[1]
    first = section == 0
    at = jnp.reshape(shard, (1,)).astype(jnp.int32)

    def by_layer(mine):
        other = swap_section(mine)
        return (jnp.where(first, mine, other), jnp.where(first, other, mine))

    x_own = lax.dynamic_index_in_dim(inputs, section, 0, keepdims=False)
    cot_own = lax.dynamic_index_in_dim(cotangent, section, 0, keepdims=False)
    seg = lax.dynamic_index_in_dim(segments, section, 0, keepdims=False)

    packed = by_layer(jnp.concatenate([attn_q[0], attn_k[0], attn_v[0], attn_out[0]], axis=1))
    half = width // 2

    def gather_weights(shard_l):
        mine = lax.dynamic_slice_in_dim(shard_l, section * half, half, 0)
        got = jnp.stack([to_ahead(mine, r) for r in range(1, n)])
        other = swap_section(got)
        low = jnp.where(first, got, other)
        high = jnp.where(first, other, got)
        return jnp.concatenate([shard_l[None], jnp.concatenate([low, high], axis=1)], axis=0)

    gains = by_layer(norm_gains[0])
    gates = by_layer(ffn_gate[0])
    ups = by_layer(ffn_up[0])
    downs = by_layer(ffn_down[0])
    u0 = gather_rows(x_own)
    weights = [gather_weights(packed[0]), gather_weights(packed[1])]
    cot = gather_rows(cot_own)

    index = jnp.arange(row_len, dtype=jnp.int32)
    pos = lax.rem(index + shard * block, row_len)
    seg_turned = lax.dynamic_slice_in_dim(jnp.concatenate([seg, seg]), shard * block, row_len, 0)
    start = jnp.sum((seg[None, :] < seg_turned[:, None]).astype(jnp.int32), axis=1)
    places = (pos - start).astype(F32)
    lane = jnp.arange(2 * HD, dtype=jnp.int32)
    frequency = rope_base ** ((lane % (HD // 2)).astype(F32) * (-2.0 / HD))
    angles = places[:, None] * frequency[None, :]
    cosine = jnp.cos(angles)
    sine = jnp.where((lane % HD < HD // 2)[None, :], -jnp.sin(angles), jnp.sin(angles))
    tables = (cosine, sine, seg_turned[:, None], pos[:, None], seg_turned[None, :], pos[None, :])

    us = [u0, None]
    saved = []
    acts = []
    for layer in range(2):
        kept = run_forward(at, us[layer], weights[layer], gates[layer], ups[layer], downs[layer], gains[layer], tables)
        saved.append(kept)
        own_out = (kept[7][:block] + scatter_rows(kept[0])).astype(BF16)
        acts.append(own_out)
        if layer == 0:
            us[1] = gather_rows(own_out)

    upstream = cot
    upstream_own = cot_own
    grads = [None, None]
    gain_parts = [None, None]
    d_inputs = [None, None]
    for layer in (1, 0):
        _, normed, q, k, v, prob, att, mid, nffn, gpre, upre, hid = saved[layer]
        dgu, part = run_ffn_back(upstream, gpre, upre, gates[layer], ups[layer], downs[layer])
        d_nffn = scatter_rows(part)
        mid_own = mid[:block]
        inv_f = lax.rsqrt(jnp.mean(mid_own * mid_own, axis=-1, keepdims=True) + epsilon)
        scaled = d_nffn * gains[layer][1]
        d_mid_own = (
            upstream_own.astype(F32)
            + inv_f * scaled
            - mid_own * (inv_f * inv_f * inv_f) * jnp.mean(scaled * mid_own, axis=-1, keepdims=True)
        ).astype(BF16)
        gain_ffn = jnp.sum(d_nffn * mid_own * inv_f, axis=0, keepdims=True)
        d_mid = gather_rows(d_mid_own)
        g_ffn = jnp.concatenate([dot_tn(nffn, dgu), dot_tn(upstream, hid)], axis=1).astype(BF16)
        red_ffn = reduce_grad(g_ffn, layer)
        d_in, dqkv, dmo, gain_attn = run_attn_back(
            at, d_mid, us[layer], weights[layer], gains[layer], cosine, sine, q, k, v, prob, att, block
        )
        g_attn = jnp.concatenate([dot_tn(normed, dqkv), dot_tn(att, dmo)], axis=1).astype(BF16)
        red_attn = reduce_grad(g_attn, layer)
        grads[layer] = (red_ffn, red_attn)
        gain_parts[layer] = jnp.concatenate([gain_attn, gain_ffn], axis=0)
        upstream = d_in
        upstream_own = d_in[:block]
        d_inputs[layer] = upstream_own

    gain_sum = jnp.concatenate(gain_parts, axis=0)
    for axis in ("section", "shard", "replica"):
        gain_sum = doubled_sum(gain_sum, axis)
    final_gains = jnp.where(first, gain_sum[:2], gain_sum[2:])
    red_ffn = jnp.where(first, grads[0][0], grads[1][0])
    red_attn = jnp.where(first, grads[0][1], grads[1][1])
    ff = ffn_gate.shape[2]
    qw = attn_q.shape[2]
    kw = attn_k.shape[2]

    def both_rows(pair):
        other = swap_section(jnp.where(first, pair[1], pair[0]))
        mine = jnp.where(first, pair[0], pair[1])
        return jnp.where(first, jnp.stack([mine, other]), jnp.stack([other, mine]))

    return (
        both_rows(acts)[None],
        both_rows(d_inputs)[None],
        red_attn[None, :, :qw],
        red_attn[None, :, qw : qw + kw],
        red_attn[None, :, qw + kw : qw + 2 * kw],
        red_attn[None, :, qw + 2 * kw :],
        red_ffn[None, :, :ff],
        red_ffn[None, :, ff : 2 * ff],
        red_ffn[:, 2 * ff :].T[None],
        final_gains[None],
    )


def solution(mesh):
    placed = (
        P("replica", "shard", None),
        P("replica", "shard", None),
        P("replica", None),
        P("section", None, "shard"),
        P("section", None, "shard"),
        P("section", None, "shard"),
        P("section", None, "shard"),
        P("section", None, "shard"),
        P("section", None, "shard"),
        P("section", "shard", None),
        P("section", None, None),
    )
    return jax.shard_map(
        local,
        mesh=mesh,
        in_specs=placed,
        out_specs=(
            P("section", "replica", "shard", None),
            P("section", "replica", "shard", None),
            P("section", "replica", "shard"),
            P("section", "replica", "shard"),
            P("section", "replica", "shard"),
            P("section", "replica", "shard"),
            P("section", "replica", "shard"),
            P("section", "replica", "shard"),
            P("section", "shard", "replica"),
            P("section", None, None),
        ),
        check_vma=False,
    )
```
